256 devices in a mesh: section: 8 (over z_lo, x), replica: 32 (over y, z_hi, core).
Axes of the slice: x: 4, y: 4, z: 8 (z_hi: 4, z_lo: 2; z = z_hi * 2 + z_lo), core: 2. Of those that a mesh axis runs over, the one named last changes fastest.
Arguments:
- inputs: bfloat16 [32, 2, 64, 2048], P('replica', None, 'section'), may hold values from -6 to 6
- cotangent: bfloat16 [32, 2, 64, 2048], P('replica', None, 'section'), may hold values from -6 to 6
- gate_weight: bfloat16 [8, 32, 2048, 768], P('section', 'replica'), may hold values from -0.125 to 0.125
- up_weight: bfloat16 [8, 32, 2048, 768], P('section', 'replica'), may hold values from -0.125 to 0.125
- down_weight: bfloat16 [8, 32, 768, 2048], P('section', 'replica'), may hold values from -0.21875 to 0.21875
- momentum: float32 [8, 32, 128, 768], P('section', 'replica'), may hold values from -6 to 6
- routes: int32 [7, 2, 32], replicated, may hold values from 0 to 31, each once within a row
- pairing: int32 [8, 32], replicated, may hold values from 0 to 31, as said below
Outputs:
- activations: bfloat16 [8, 32, 2, 64, 2048], P('section', 'replica')
- input_grads: bfloat16 [8, 32, 2, 64, 2048], P('section', 'replica')
- buckets: float32 [8, 32, 128, 768], P('section', 'replica')
The draws below stay inside these ranges and needn't reach their ends.
Inputs may be any that keep to these rules, and one draw needn't show every extreme that they name: routes[s, m] is a permutation of the 32 replicas. pairing[s] splits the 32 replicas into pairs: pairing[s, pairing[s, r]] = r and pairing[s, r] != r.
All inputs are finite; a program needn't handle non-finite values.
Results may differ from the reference program's by a relative error of at most 0.028.
Values may be sent and summed in bfloat16 or wider, within the bound.
A program may use at most 64 MiB of HBM per device.

```python
import jax
import jax.numpy as jnp
from jax import lax

D = 2048
FF = 768
ROWS = 64
MICRO = 2
BUCKET = 128
SECTIONS = 8
REPLICAS = 32


def draw_pairing(key, part):
    keys = jax.random.split(jax.random.fold_in(key, 17), SECTIONS)

    def single(subkey):
        order = jax.random.permutation(subkey, REPLICAS).astype(jnp.int32)
        first = order[0::2]
        second = order[1::2]
        result = jnp.zeros((REPLICAS,), jnp.int32)
        result = result.at[first].set(second).at[second].set(first)
        return result
    return jax.vmap(single)(keys)


def levels(rng, dims, shards, least, high):
    level = 1.0
    for dim, shards_of in shards:
        draws = jax.random.uniform(jax.random.fold_in(jax.random.fold_in(rng, 6), dim), (shards_of,), jnp.float32, least / len(shards), high / len(shards))
        level = level * jnp.repeat(jnp.exp(draws), dims[dim] // shards_of).reshape((-1,) + (1,) * (len(dims) - 1 - dim))
    return level


def noise(stream_key, extent, width, limit, shards=(), kind=jnp.bfloat16):
    values = jax.random.normal(stream_key, extent, jnp.float32) * width
    if len(shards) > 0:
        values = levels(stream_key, extent, shards, -0.22, 0.18) * values
    return jnp.clip(values, min=-limit, max=limit).astype(kind)


def setup_inputs(seed: int = 0) -> dict:
    key_list = jax.random.split(jax.random.key(seed), 9)
    inputs = noise(key_list[0], (REPLICAS, MICRO, ROWS, D), 1.0, 6.0, ((0, 32), (2, 8)))
    cotangent = noise(key_list[1], (REPLICAS, MICRO, ROWS, D), 1.0, 6.0, ((0, 32), (2, 8)))
    gate_weight = noise(key_list[2], (SECTIONS, REPLICAS, D, FF), D ** -0.5, 0.125, ((0, 8), (1, 32)))
    up_weight = noise(key_list[3], (SECTIONS, REPLICAS, D, FF), D ** -0.5, 0.125, ((0, 8), (1, 32)))
    down_weight = noise(key_list[4], (SECTIONS, REPLICAS, FF, D), FF ** -0.5, 0.21875, ((0, 8), (1, 32)))
    momentum = noise(key_list[5], (SECTIONS, REPLICAS, BUCKET, FF), 1.0, 6.0, ((0, 8), (1, 32)), jnp.float32)
    routes = jax.vmap(lambda own: jax.random.permutation(own, REPLICAS))(jax.random.split(key_list[6], (SECTIONS - 1) * MICRO)).reshape((SECTIONS - 1, MICRO, REPLICAS)).astype(jnp.int32)
    pairing = draw_pairing(jax.random.fold_in(key_list[8], 71), 0)
    return {"inputs": inputs, "cotangent": cotangent, "gate_weight": gate_weight, "up_weight": up_weight, "down_weight": down_weight, "momentum": momentum, "routes": routes, "pairing": pairing}


EPS = 1e-06
BETA = 0.9

def normalize(af):
    rinv = lax.rsqrt(lax.optimization_barrier(jnp.mean(af * af, axis=-1, keepdims=True)) + EPS)
    return (af * rinv, rinv)

def expert_forward(block, gate, up, down):
    af = block.astype(jnp.float32)
    normed, rinv = normalize(af)
    narrow = normed.astype(jnp.bfloat16)
    gated = jnp.dot(narrow, gate, preferred_element_type=jnp.float32)
    upward = jnp.dot(narrow, up, preferred_element_type=jnp.float32)
    hidden = (jax.nn.silu(gated) * upward).astype(jnp.bfloat16)
    return (af + jnp.dot(hidden, down, preferred_element_type=jnp.float32)).astype(jnp.bfloat16)

def expert_backward(block, dout, gate, up, down):
    af = block.astype(jnp.float32)
    normed, rinv = normalize(af)
    narrow = normed.astype(jnp.bfloat16)
    gated = jnp.dot(narrow, gate, preferred_element_type=jnp.float32)
    upward = jnp.dot(narrow, up, preferred_element_type=jnp.float32)
    sigma = jax.nn.sigmoid(gated)
    dhidden = jnp.dot(dout, down.T, preferred_element_type=jnp.float32)
    dgate = (dhidden * upward * sigma * (1.0 + gated * (1.0 - sigma))).astype(jnp.bfloat16)
    dup = (dhidden * gated * sigma).astype(jnp.bfloat16)
    dnorm = jnp.dot(dgate, gate.T, preferred_element_type=jnp.float32) + jnp.dot(dup, up.T, preferred_element_type=jnp.float32)
    dinput = dout.astype(jnp.float32) + rinv * (dnorm - normed * lax.optimization_barrier(jnp.mean(dnorm * normed, axis=-1, keepdims=True)))
    part = jnp.dot(narrow[:, :BUCKET].T, dgate, preferred_element_type=jnp.float32)
    return (dinput.astype(jnp.bfloat16), part)

def reference(inputs, cotangent, gate_weight, up_weight, down_weight, momentum, routes, pairing):
    forward_all = jax.vmap(jax.vmap(expert_forward, (0, None, None, None)), (0, 0, 0, 0))
    backward_all = jax.vmap(jax.vmap(expert_backward, (0, 0, None, None, None)), (0, 0, 0, 0, 0))
    series = jnp.arange(REPLICAS, dtype=jnp.int32)
    section_in = []
    outs = []
    current = inputs
    for section in range(SECTIONS):
        section_in.append(current)
        result = forward_all(current, gate_weight[section], up_weight[section], down_weight[section])
        outs.append(result)
        if section + 1 < SECTIONS:
            moved = []
            for micro in range(MICRO):
                inverse = jnp.zeros((REPLICAS,), jnp.int32).at[routes[section, micro]].set(series)
                moved.append(result[inverse, micro])
            current = jnp.stack(moved, axis=1)
    grads = [None] * SECTIONS
    buckets = [None] * SECTIONS
    dout = cotangent
    for section in range(SECTIONS - 1, -1, -1):
        dinput, parts = backward_all(section_in[section], dout, gate_weight[section], up_weight[section], down_weight[section])
        grads[section] = dinput
        total = lax.optimization_barrier(jnp.sum(parts, axis=1))
        fresh = (BETA * momentum[section] + (1.0 - BETA) * total).astype(jnp.bfloat16)
        fresh = lax.optimization_barrier(fresh).astype(jnp.float32)
        buckets[section] = 0.5 * (fresh + fresh[pairing[section]])
        if section > 0:
            moved = []
            for micro in range(MICRO):
                moved.append(dinput[routes[section - 1, micro], micro])
            dout = jnp.stack(moved, axis=1)
    return (jnp.stack(outs), jnp.stack(grads), jnp.stack(buckets))
```

```python
import jax
import jax.numpy as jnp
from jax import lax
from jax.experimental import pallas as pl
from jax.experimental.pallas import tpu as pltpu
from jax.sharding import PartitionSpec as P

EPS = 1e-06
BETA = 0.9
MESH = pl.DeviceIdType.MESH
F32, BF16 = jnp.float32, jnp.bfloat16
SECTIONS, REPLICAS, MICRO, ROWS, D, FF, BUCKET = 8, 32, 2, 64, 2048, 768, 128
PR, PC = 32, 128
CHUNK = 256
BP = (BUCKET // PR) * (FF // PC)


def contract_last(a, b):
    return lax.dot_general(a, b, (((1,), (1,)), ((), ())), preferred_element_type=F32)


def kernel(inp, cot, gate_h, up_h, down_h, mom_h, routes_v, routes_s, pairing_s,
           act_h, ig_h, buck_h,
           gate, up, down, mom, gx, xd, out, p1a, p1b, p1c, p1d, p1e, snd, nbuf, rinv_b, g_b, u_b, a_b, b_b, total,
           fresh, partner, bucket, inv_v, inv_s,
           w_sem, m_sem, g_sem, gs_sem, p1_recv, p1_send, p2_recv, p2_send, o_sem, i_sem):
    t = lax.axis_index("section")
    r = lax.axis_index("replica")
    p1 = (p1a, p1b, p1c, p1d, p1e)
    relay_at = lax.rem(t + 4, SECTIONS)
    source = lax.rem(t + 4, SECTIONS)

    def dev(s, q):
        return {"section": s, "replica": q}

    def wait(ref, sem):
        pltpu.make_async_copy(ref, ref, sem).wait()

    loads = [pltpu.make_async_copy(h, v, w_sem.at[i])
             for i, (h, v) in enumerate(((gate_h.at[0, 0], gate), (up_h.at[0, 0], up), (down_h.at[0, 0], down)))]

    def gather(src, goal, sems):
        @pl.when(t == goal)
        def _():
            for m in range(MICRO):
                pltpu.make_async_copy(src.at[0, m], gx.at[m, t], g_sem.at[m]).start()

        @pl.when(t != goal)
        def _():
            for m in range(MICRO):
                pltpu.make_async_remote_copy(
                    src.at[0, m], gx.at[m, t], gs_sem.at[sems + m], g_sem.at[m],
                    device_id=dev(goal, r), device_id_type=MESH).start()

    gather(inp, 0, 0)
    for load in loads:
        load.start()
    gather(cot, SECTIONS - 1, MICRO)
    pltpu.make_async_copy(mom_h.at[0, 0], mom, m_sem).start()

    rv = routes_v[jnp.minimum(source, SECTIONS - 2)]
    goal_id = lax.broadcasted_iota(jnp.int32, (REPLICAS, REPLICAS), 0)
    from_id = lax.broadcasted_iota(jnp.int32, (REPLICAS, REPLICAS), 1)
    for m in range(MICRO):
        hit = rv[m:m + 1, :] == goal_id
        back = jnp.max(jnp.where(hit, from_id, 0), axis=1, keepdims=True)
        inv_v[m] = jnp.broadcast_to(back, (REPLICAS, 128))
    copy = pltpu.make_async_copy(inv_v, inv_s, i_sem)
    copy.start()
    copy.wait()

    def assemble(m, slot):
        wait(gx.at[m], g_sem.at[m])
        for k in range(SECTIONS):
            xd[slot, pl.ds(8 * k, 8), :] = gx[m, k]

    def send_chunk(slot, c0):
        for c in range(c0, c0 + CHUNK // PC):
            for h in range(ROWS // PR):
                q = c * (ROWS // PR) + h
                pltpu.make_async_remote_copy(
                    out.at[slot, pl.ds(h * PR, PR), pl.ds(c * PC, PC)],
                    p1[slot].at[r], p1_send.at[slot], p1_recv.at[slot],
                    device_id=dev(relay_at, q), device_id_type=MESH).start()

    def forward(m):
        @pl.when(t == 0)
        def _():
            assemble(m, m)

        @pl.when(t != 0)
        def _():
            wait(xd.at[m], p2_recv.at[m])

        af = xd[m].astype(F32)
        rinv = lax.rsqrt(jnp.mean(af * af, axis=-1, keepdims=True) + EPS)
        rinv_b[m] = jnp.broadcast_to(rinv, (ROWS, 128))
        nb = (af * rinv).astype(BF16)
        nbuf[m] = nb[:, :BUCKET]

        if m == 0:
            loads[0].wait()
            loads[1].wait()

        g = jnp.dot(nb, gate[...], preferred_element_type=F32)
        u = jnp.dot(nb, up[...], preferred_element_type=F32)
        sg = jax.nn.sigmoid(g)
        gs = g * sg
        hidden = (gs * u).astype(BF16)

        if m == 0:
            loads[2].wait()

        for c in range(0, D, CHUNK):
            res = xd[m, :, pl.ds(c, CHUNK)].astype(F32) + jnp.dot(
                hidden, down[:, pl.ds(c, CHUNK)], preferred_element_type=F32)
            out[m, :, pl.ds(c, CHUNK)] = res.astype(BF16)

            @pl.when(t < SECTIONS - 1)
            def _():
                send_chunk(m, c // PC)

        pltpu.make_async_copy(out.at[m], act_h.at[0, 0, m], o_sem).start()
        g_b[m] = g
        u_b[m] = u
        a_b[m] = u * sg * (1.0 + g * (1.0 - sg))
        b_b[m] = gs

    def backward(m):
        slot = MICRO + m

        @pl.when(t == SECTIONS - 1)
        def _():
            assemble(m, slot)

        @pl.when(t != SECTIONS - 1)
        def _():
            wait(xd.at[slot], p2_recv.at[slot])

        dout = xd[slot]
        dh = contract_last(dout, down[...])
        dg = (dh * a_b[m]).astype(BF16)
        du = (dh * b_b[m]).astype(BF16)
        both = dg.astype(F32) * g_b[m] + du.astype(F32) * u_b[m]
        corr = jnp.sum(both, axis=-1, keepdims=True) * (1.0 / D)
        rinv = rinv_b[m][:, :1]
        for c in range(0, D, CHUNK):
            dn = contract_last(dg, gate[pl.ds(c, CHUNK), :]) + contract_last(du, up[pl.ds(c, CHUNK), :])
            n = xd[m, :, pl.ds(c, CHUNK)].astype(F32) * rinv
            res = xd[slot, :, pl.ds(c, CHUNK)].astype(F32) + rinv * (dn - n * corr)
            out[slot, :, pl.ds(c, CHUNK)] = res.astype(BF16)

            @pl.when(t > 0)
            def _():
                send_chunk(slot, c // PC)

        pltpu.make_async_copy(out.at[slot], ig_h.at[0, 0, m], o_sem).start()
        part = lax.dot_general(nbuf[m], dg, (((0,), (0,)), ((), ())), preferred_element_type=F32)

        total[...] = part if m == 0 else total[...] + part

    half = lax.rem(r, ROWS // PR)
    col = r // (ROWS // PR)

    def relay(slot, goal, index):
        wait(p1[slot], p1_recv.at[slot])
        place = xd.at[slot, pl.ds(pl.multiple_of(half * PR, PR), PR), pl.ds(pl.multiple_of(col * PC, PC), PC)]

        def body(d, carry):
            snd[slot, d] = p1[slot][index(d)]
            pltpu.make_async_remote_copy(
                snd.at[slot, d], place, p2_send.at[slot], p2_recv.at[slot],
                device_id=dev(goal, d), device_id_type=MESH).start()
            return carry

        lax.fori_loop(0, REPLICAS, body, 0)

    def relay_forward():
        @pl.when(source < SECTIONS - 1)
        def _():
            for m in range(MICRO):
                relay(m, source + 1, lambda d: inv_s[m, d, 0])

    def relay_backward():
        @pl.when(source > 0)
        def _():
            for m in range(MICRO):
                relay(MICRO + m, source - 1, lambda d: routes_s[source - 1, m, d])

        @pl.when(r < BP)
        def _():
            slot = 2 * MICRO
            wait(p1[slot], p1_recv.at[slot])
            brow, bcol = r // (FF // PC), lax.rem(r, FF // PC)
            place = partner.at[pl.ds(pl.multiple_of(brow * PR, PR), PR), pl.ds(pl.multiple_of(bcol * PC, PC), PC)]

            def body(d, carry):
                snd[slot, d] = p1[slot][pairing_s[source, d]]
                pltpu.make_async_remote_copy(
                    snd.at[slot, d], place, p2_send.at[slot], p2_recv.at[slot],
                    device_id=dev(source, d), device_id_type=MESH).start()
                return carry

            lax.fori_loop(0, REPLICAS, body, 0)

    early = t < SECTIONS // 2

    @pl.when(jnp.logical_not(early))
    def _():
        relay_forward()

    for m in range(MICRO):
        forward(m)

    @pl.when(early)
    def _():
        relay_forward()
        relay_backward()

    for m in range(MICRO):
        backward(m)

    wait(mom, m_sem)
    fresh[...] = (BETA * mom[...] + (1.0 - BETA) * total[...]).astype(BF16)
    for q in range(BP):
        pltpu.make_async_remote_copy(
            fresh.at[pl.ds(q // (FF // PC) * PR, PR), pl.ds(q % (FF // PC) * PC, PC)],
            p1[2 * MICRO].at[r], p1_send.at[2 * MICRO], p1_recv.at[2 * MICRO],
            device_id=dev(relay_at, q), device_id_type=MESH).start()

    @pl.when(jnp.logical_not(early))
    def _():
        relay_backward()

    wait(partner, p2_recv.at[2 * MICRO])
    bucket[...] = 0.5 * (fresh[...].astype(F32) + partner[...].astype(F32))
    pltpu.make_async_copy(bucket, buck_h.at[0, 0], m_sem).start()

    wait(fresh, p1_send.at[2 * MICRO])

    @pl.when(r < BP)
    def _():
        wait(snd.at[2 * MICRO], p2_send.at[2 * MICRO])

    @pl.when(t < SECTIONS - 1)
    def _():
        for m in range(MICRO):
            wait(out.at[m], p1_send.at[m])

    @pl.when(t > 0)
    def _():
        for m in range(MICRO):
            wait(out.at[MICRO + m], p1_send.at[MICRO + m])

    @pl.when(source < SECTIONS - 1)
    def _():
        for m in range(MICRO):
            wait(snd.at[m], p2_send.at[m])

    @pl.when(source > 0)
    def _():
        for m in range(MICRO):
            wait(snd.at[MICRO + m], p2_send.at[MICRO + m])

    def sent(src, sems):
        for m in range(MICRO):
            pltpu.make_async_remote_copy(
                src.at[0, m], gx.at[m, t], gs_sem.at[sems + m], g_sem.at[m],
                device_id=dev(0, r), device_id_type=MESH).wait_send()

    @pl.when(t != 0)
    def _():
        sent(inp, 0)

    @pl.when(t != SECTIONS - 1)
    def _():
        sent(cot, MICRO)

    wait(out, o_sem)
    wait(bucket, m_sem)


def local(inputs, cotangent, gate_weight, up_weight, down_weight, momentum, routes, pairing):
    hbm = pl.BlockSpec(memory_space=pl.ANY)
    smem = pl.BlockSpec(memory_space=pltpu.SMEM)
    vmem = pl.BlockSpec(memory_space=pltpu.VMEM)
    dma = pltpu.SemaphoreType.DMA
    slots = 2 * MICRO
    return pl.pallas_call(
        kernel,
        out_shape=(
            jax.ShapeDtypeStruct((1, 1, MICRO, ROWS, D), BF16),
            jax.ShapeDtypeStruct((1, 1, MICRO, ROWS, D), BF16),
            jax.ShapeDtypeStruct((1, 1, BUCKET, FF), F32),
        ),
        in_specs=[hbm] * 6 + [vmem, smem, smem],
        out_specs=(hbm, hbm, hbm),
        scratch_shapes=[
            pltpu.VMEM((D, FF), BF16),
            pltpu.VMEM((D, FF), BF16),
            pltpu.VMEM((FF, D), BF16),
            pltpu.VMEM((BUCKET, FF), F32),
            pltpu.VMEM((MICRO, SECTIONS, ROWS // SECTIONS, D), BF16),
            pltpu.VMEM((slots, ROWS, D), BF16),
            pltpu.VMEM((slots, ROWS, D), BF16),
            *[pltpu.VMEM((REPLICAS, PR, PC), BF16)] * (slots + 1),
            pltpu.VMEM((slots + 1, REPLICAS, PR, PC), BF16),
            pltpu.VMEM((MICRO, ROWS, BUCKET), BF16),
            pltpu.VMEM((MICRO, ROWS, 128), F32),
            pltpu.VMEM((MICRO, ROWS, FF), F32),
            pltpu.VMEM((MICRO, ROWS, FF), F32),
            pltpu.VMEM((MICRO, ROWS, FF), F32),
            pltpu.VMEM((MICRO, ROWS, FF), F32),
            pltpu.VMEM((BUCKET, FF), F32),
            pltpu.VMEM((BUCKET, FF), BF16),
            pltpu.VMEM((BUCKET, FF), BF16),
            pltpu.VMEM((BUCKET, FF), F32),
            pltpu.VMEM((MICRO, REPLICAS, 128), jnp.int32),
            pltpu.SMEM((MICRO, REPLICAS, 128), jnp.int32),
            dma((3,)),
            dma,
            dma((MICRO,)),
            dma((2 * MICRO,)),
            dma((slots + 1,)),
            dma((slots + 1,)),
            dma((slots + 1,)),
            dma((slots + 1,)),
            dma,
            dma,
        ],
        compiler_params=pltpu.CompilerParams(has_side_effects=True, vmem_limit_bytes=56 << 20),
    )(inputs, cotangent, gate_weight, up_weight, down_weight, momentum, routes, routes, pairing)


def solution(mesh):
    placed = (
        P("replica", None, "section", None),
        P("replica", None, "section", None),
        P("section", "replica", None, None),
        P("section", "replica", None, None),
        P("section", "replica", None, None),
        P("section", "replica", None, None),
        P(),
        P(),
    )
    return jax.shard_map(
        local,
        mesh=mesh,
        in_specs=placed,
        out_specs=(
            P("section", "replica", None, None, None),
            P("section", "replica", None, None, None),
            P("section", "replica", None, None),
        ),
        check_vma=False,
    )
```

```python
import jax
import jax.numpy as jnp
from jax import lax
from jax.experimental import pallas as pl
from jax.experimental.pallas import tpu as pltpu
from jax.sharding import PartitionSpec as P

EPS = 1e-06
BETA = 0.9
MESH = pl.DeviceIdType.MESH
F32, BF16 = jnp.float32, jnp.bfloat16
SECTIONS, REPLICAS, MICRO, ROWS, D, FF, BUCKET = 8, 32, 2, 64, 2048, 768, 128
PR, PC = 32, 128
CHUNK = 256
GROUPS = 4
SPAN = D // GROUPS
BP = (BUCKET // PR) * (FF // PC)


def kernel(inp, cot, gate_h, up_h, down_h, mom_h, routes_v, routes_s, pairing_s,
           act_h, ig_h, buck_h,
           gate, up, down, mom, gx, xd, out, p1a, p1b, p1c, p1d, p1e, snd, nbuf, rinv_b, g_b, u_b, a_b, b_b, total,
           fresh, partner, bucket, inv_v, inv_s,
           gate_t, up_t, down_t,
           w_sem, m_sem, g_sem, gs_sem, p1_recv, p1_send, p2_recv, b_recv, p2_send, o_sem, i_sem):
    t = lax.axis_index("section")
    r = lax.axis_index("replica")
    p1 = (p1a, p1b, p1c, p1d, p1e)
    across = lax.rem(t + 4, SECTIONS)
    core, ry, rz = lax.rem(r, 2), r // 8, lax.rem(r, 8) // 2
    group = lax.rem(rz - ry + 4, 4)
    half = lax.rem(ry, ROWS // PR)
    col = 2 * (2 * group + core) + ry // (ROWS // PR)
    fwd_source = lax.rem(t + 4 - core, SECTIONS)
    bwd_source = lax.rem(t + 4 + core, SECTIONS)

    def dev(s, q):
        return {"section": s, "replica": q}

    def wait(ref, sem):
        pltpu.make_async_copy(ref, ref, sem).wait()

    early = t < SECTIONS // 2

    loads = [pltpu.make_async_copy(h, v, w_sem.at[i])
             for i, (h, v) in enumerate(((gate_h.at[0, 0], gate), (up_h.at[0, 0], up), (down_h.at[0, 0], down)))]

    def gather(src, goal, sems):
        @pl.when(t == goal)
        def _():
            for m in range(MICRO):
                pltpu.make_async_copy(src.at[0, m], gx.at[m, t], g_sem.at[m]).start()

        @pl.when(t != goal)
        def _():
            for m in range(MICRO):
                pltpu.make_async_remote_copy(
                    src.at[0, m], gx.at[m, t], gs_sem.at[sems + m], g_sem.at[m],
                    device_id=dev(goal, r), device_id_type=MESH).start()

    gather(inp, 0, 0)
    for load in loads:
        load.start()
    gather(cot, SECTIONS - 1, MICRO)
    pltpu.make_async_copy(mom_h.at[0, 0], mom, m_sem).start()

    rv = routes_v[jnp.minimum(fwd_source, SECTIONS - 2)]
    goal_id = lax.broadcasted_iota(jnp.int32, (REPLICAS, REPLICAS), 0)
    from_id = lax.broadcasted_iota(jnp.int32, (REPLICAS, REPLICAS), 1)
    for m in range(MICRO):
        hit = rv[m:m + 1, :] == goal_id
        back = jnp.max(jnp.where(hit, from_id, 0), axis=1, keepdims=True)
        inv_v[m] = jnp.broadcast_to(back, (REPLICAS, 128))
    copy = pltpu.make_async_copy(inv_v, inv_s, i_sem)
    copy.start()
    copy.wait()

    def assemble(m, slot):
        wait(gx.at[m], g_sem.at[m])
        for k in range(SECTIONS):
            xd[slot, pl.ds(8 * k, 8), :] = gx[m, k]

    def send_chunk(slot, j):
        step = 1 if slot < MICRO else -1
        at = across if j % 2 == 0 else lax.rem(t + 4 + step, SECTIONS)
        for k in range(4):
            c, h = 2 * j + k // 2, k % 2
            q = k * 8 + (j // 2 + k) % 4 * 2 + j % 2
            pltpu.make_async_remote_copy(
                out.at[slot, pl.ds(h * PR, PR), pl.ds(c * PC, PC)],
                p1[slot].at[r], p1_send.at[slot], p1_recv.at[slot],
                device_id=dev(at, q), device_id_type=MESH).start()

    def forward(m):
        @pl.when(t == 0)
        def _():
            assemble(m, m)

        if m == 0:
            @pl.when(early)
            def _():
                loads[0].wait()
                loads[1].wait()

        squares = jnp.zeros((ROWS, 128), F32)
        g = jnp.zeros((ROWS, FF), F32)
        u = jnp.zeros((ROWS, FF), F32)
        for k in range(GROUPS):
            cols = pl.ds(k * SPAN, SPAN)

            @pl.when(t != 0)
            def _():
                wait(xd.at[m, :, cols], p2_recv.at[m, k])

            a = xd[m, :, cols]
            g = g + jnp.dot(a, gate[cols, :], preferred_element_type=F32)
            u = u + jnp.dot(a, up[cols, :], preferred_element_type=F32)
            for c in range(0, SPAN, 128):
                af = a[:, c:c + 128].astype(F32)
                squares = squares + af * af
        rinv = lax.rsqrt(jnp.sum(squares, axis=-1, keepdims=True) * (1.0 / D) + EPS)
        g = g * rinv
        u = u * rinv
        sg = jax.nn.sigmoid(g)
        gs = g * sg
        hidden = (gs * u).astype(BF16)

        if m == 0:
            @pl.when(early)
            def _():
                loads[2].wait()

        for c in range(0, D, CHUNK):
            res = xd[m, :, pl.ds(c, CHUNK)].astype(F32) + jnp.dot(
                hidden, down[:, pl.ds(c, CHUNK)], preferred_element_type=F32)
            out[m, :, pl.ds(c, CHUNK)] = res.astype(BF16)

            @pl.when(t < SECTIONS - 1)
            def _():
                send_chunk(m, c // CHUNK)

        pltpu.make_async_copy(out.at[m], act_h.at[0, 0, m], o_sem).start()
        rinv_b[m] = jnp.broadcast_to(rinv, (ROWS, 128))
        nbuf[m] = (xd[m, :, :BUCKET].astype(F32) * rinv).astype(BF16)
        g_b[m] = g
        u_b[m] = u
        a_b[m] = u * sg * (1.0 + g * (1.0 - sg))
        b_b[m] = gs

    def backward(m):
        slot = MICRO + m

        @pl.when(t == SECTIONS - 1)
        def _():
            assemble(m, slot)

        dh = jnp.zeros((ROWS, FF), F32)
        for k in range(GROUPS):
            cols = pl.ds(k * SPAN, SPAN)

            @pl.when(t != SECTIONS - 1)
            def _():
                wait(xd.at[slot, :, cols], p2_recv.at[slot, k])

            dh = dh + jnp.dot(xd[slot, :, cols], down_t[cols, :], preferred_element_type=F32)
        dg = (dh * a_b[m]).astype(BF16)
        du = (dh * b_b[m]).astype(BF16)
        both = dg.astype(F32) * g_b[m] + du.astype(F32) * u_b[m]
        corr = jnp.sum(both, axis=-1, keepdims=True) * (1.0 / D)
        rinv = rinv_b[m][:, :1]
        for c in range(0, D, CHUNK):
            cols = pl.ds(c, CHUNK)
            dn = jnp.dot(dg, gate_t[:, cols], preferred_element_type=F32) + jnp.dot(
                du, up_t[:, cols], preferred_element_type=F32)
            n = xd[m, :, pl.ds(c, CHUNK)].astype(F32) * rinv
            res = xd[slot, :, pl.ds(c, CHUNK)].astype(F32) + rinv * (dn - n * corr)
            out[slot, :, pl.ds(c, CHUNK)] = res.astype(BF16)

            @pl.when(t > 0)
            def _():
                send_chunk(slot, c // CHUNK)

        pltpu.make_async_copy(out.at[slot], ig_h.at[0, 0, m], o_sem).start()
        part = lax.dot_general(nbuf[m], dg, (((0,), (0,)), ((), ())), preferred_element_type=F32)

        total[...] = part if m == 0 else total[...] + part

    def relay(slot, goal, index):
        wait(p1[slot], p1_recv.at[slot])
        place = xd.at[slot, pl.ds(pl.multiple_of(half * PR, PR), PR), pl.ds(pl.multiple_of(col * PC, PC), PC)]

        def body(d, carry):
            snd[slot, d] = p1[slot][index(d)]
            pltpu.make_async_remote_copy(
                snd.at[slot, d], place, p2_send.at[slot], p2_recv.at[slot, group],
                device_id=dev(goal, d), device_id_type=MESH).start()
            return carry

        lax.fori_loop(0, REPLICAS, body, 0, unroll=4)

    def relay_forward():
        @pl.when(fwd_source < SECTIONS - 1)
        def _():
            for m in range(MICRO):
                relay(m, fwd_source + 1, lambda d: inv_s[m, d, 0])

    def relay_backward():
        @pl.when(bwd_source > 0)
        def _():
            for m in range(MICRO):
                relay(MICRO + m, bwd_source - 1, lambda d: routes_s[bwd_source - 1, m, d])

    def relay_bucket():
        @pl.when(r < BP)
        def _():
            slot = 2 * MICRO
            wait(p1[slot], p1_recv.at[slot])
            brow, bcol = r // (FF // PC), lax.rem(r, FF // PC)
            place = partner.at[pl.ds(pl.multiple_of(brow * PR, PR), PR), pl.ds(pl.multiple_of(bcol * PC, PC), PC)]

            def body(d, carry):
                snd[slot, d] = p1[slot][pairing_s[across, d]]
                pltpu.make_async_remote_copy(
                    snd.at[slot, d], place, p2_send.at[slot], b_recv,
                    device_id=dev(across, d), device_id_type=MESH).start()
                return carry

            lax.fori_loop(0, REPLICAS, body, 0)

    def transpose():
        def body(i, carry):
            cols = pl.ds(pl.multiple_of(i * CHUNK, CHUNK), CHUNK)
            gate_t[:, cols] = gate[cols, :].T
            up_t[:, cols] = up[cols, :].T
            down_t[cols, :] = down[:, cols].T
            return carry

        lax.fori_loop(0, D // CHUNK, body, 0)

    @pl.when(jnp.logical_not(early))
    def _():
        relay_forward()
        for load in loads:
            load.wait()
        transpose()

    for m in range(MICRO):
        forward(m)

    @pl.when(early)
    def _():
        transpose()
        relay_forward()
        relay_backward()
        relay_bucket()

    for m in range(MICRO):
        backward(m)

    wait(mom, m_sem)
    fresh[...] = (BETA * mom[...] + (1.0 - BETA) * total[...]).astype(BF16)
    for q in range(BP):
        pltpu.make_async_remote_copy(
            fresh.at[pl.ds(q // (FF // PC) * PR, PR), pl.ds(q % (FF // PC) * PC, PC)],
            p1[2 * MICRO].at[r], p1_send.at[2 * MICRO], p1_recv.at[2 * MICRO],
            device_id=dev(across, q), device_id_type=MESH).start()

    @pl.when(jnp.logical_not(early))
    def _():
        relay_backward()
        relay_bucket()

    wait(partner, b_recv)
    bucket[...] = 0.5 * (fresh[...].astype(F32) + partner[...].astype(F32))
    pltpu.make_async_copy(bucket, buck_h.at[0, 0], m_sem).start()

    wait(fresh, p1_send.at[2 * MICRO])

    @pl.when(r < BP)
    def _():
        wait(snd.at[2 * MICRO], p2_send.at[2 * MICRO])

    @pl.when(t < SECTIONS - 1)
    def _():
        for m in range(MICRO):
            wait(out.at[m], p1_send.at[m])

    @pl.when(t > 0)
    def _():
        for m in range(MICRO):
            wait(out.at[MICRO + m], p1_send.at[MICRO + m])

    @pl.when(fwd_source < SECTIONS - 1)
    def _():
        for m in range(MICRO):
            wait(snd.at[m], p2_send.at[m])

    @pl.when(bwd_source > 0)
    def _():
        for m in range(MICRO):
            wait(snd.at[MICRO + m], p2_send.at[MICRO + m])

    def sent(src, sems):
        for m in range(MICRO):
            pltpu.make_async_remote_copy(
                src.at[0, m], gx.at[m, t], gs_sem.at[sems + m], g_sem.at[m],
                device_id=dev(0, r), device_id_type=MESH).wait_send()

    @pl.when(t != 0)
    def _():
        sent(inp, 0)

    @pl.when(t != SECTIONS - 1)
    def _():
        sent(cot, MICRO)

    wait(out, o_sem)
    wait(bucket, m_sem)


def hand_over(*refs):
    came, made, held, sem = refs[:3], refs[3:6], refs[6:9], refs[9]
    into = [pltpu.make_async_copy(came[i], held[i], sem.at[i]) for i in range(3)]
    away = [pltpu.make_async_copy(held[i], made[i], sem.at[3 + i]) for i in range(3)]
    for copy in into:
        copy.start()
    for i in range(3):
        into[i].wait()
        away[i].start()
    for copy in away:
        copy.wait()


def local(inputs, cotangent, gate_weight, up_weight, down_weight, momentum, routes, pairing):
    hbm = pl.BlockSpec(memory_space=pl.ANY)
    smem = pl.BlockSpec(memory_space=pltpu.SMEM)
    vmem = pl.BlockSpec(memory_space=pltpu.VMEM)
    dma = pltpu.SemaphoreType.DMA
    slots = 2 * MICRO
    made = pl.pallas_call(
        kernel,
        out_shape=(
            jax.ShapeDtypeStruct((1, 1, MICRO, ROWS, D), BF16),
            jax.ShapeDtypeStruct((1, 1, MICRO, ROWS, D), BF16),
            jax.ShapeDtypeStruct((1, 1, BUCKET, FF), F32),
        ),
        in_specs=[hbm] * 6 + [vmem, smem, smem],
        out_specs=(hbm, hbm, hbm),
        scratch_shapes=[
            pltpu.VMEM((D, FF), BF16),
            pltpu.VMEM((D, FF), BF16),
            pltpu.VMEM((FF, D), BF16),
            pltpu.VMEM((BUCKET, FF), F32),
            pltpu.VMEM((MICRO, SECTIONS, ROWS // SECTIONS, D), BF16),
            pltpu.VMEM((slots, ROWS, D), BF16),
            pltpu.VMEM((slots, ROWS, D), BF16),
            *[pltpu.VMEM((REPLICAS, PR, PC), BF16)] * (slots + 1),
            pltpu.VMEM((slots + 1, REPLICAS, PR, PC), BF16),
            pltpu.VMEM((MICRO, ROWS, BUCKET), BF16),
            pltpu.VMEM((MICRO, ROWS, 128), F32),
            pltpu.VMEM((MICRO, ROWS, FF), F32),
            pltpu.VMEM((MICRO, ROWS, FF), F32),
            pltpu.VMEM((MICRO, ROWS, FF), F32),
            pltpu.VMEM((MICRO, ROWS, FF), F32),
            pltpu.VMEM((BUCKET, FF), F32),
            pltpu.VMEM((BUCKET, FF), BF16),
            pltpu.VMEM((BUCKET, FF), BF16),
            pltpu.VMEM((BUCKET, FF), F32),
            pltpu.VMEM((MICRO, REPLICAS, 128), jnp.int32),
            pltpu.SMEM((MICRO, REPLICAS, 128), jnp.int32),
            pltpu.VMEM((FF, D), BF16),
            pltpu.VMEM((FF, D), BF16),
            pltpu.VMEM((D, FF), BF16),
            dma((3,)),
            dma,
            dma((MICRO,)),
            dma((2 * MICRO,)),
            dma((slots + 1,)),
            dma((slots + 1,)),
            dma((slots, GROUPS)),
            dma,
            dma((slots + 1,)),
            dma,
            dma,
        ],
        compiler_params=pltpu.CompilerParams(has_side_effects=True, vmem_limit_bytes=56 << 20),
    )(inputs, cotangent, gate_weight, up_weight, down_weight, momentum, routes, routes, pairing)
    return pl.pallas_call(
        hand_over,
        out_shape=tuple(jax.ShapeDtypeStruct(a.shape, a.dtype) for a in made),
        in_specs=[hbm] * 3,
        out_specs=(hbm, hbm, hbm),
        scratch_shapes=[*[pltpu.VMEM(a.shape, a.dtype) for a in made], dma((6,))],
    )(*made)


def solution(mesh):
    placed = (
        P("replica", None, "section", None),
        P("replica", None, "section", None),
        P("section", "replica", None, None),
        P("section", "replica", None, None),
        P("section", "replica", None, None),
        P("section", "replica", None, None),
        P(),
        P(),
    )
    return jax.shard_map(
        local,
        mesh=mesh,
        in_specs=placed,
        out_specs=(
            P("section", "replica", None, None, None),
            P("section", "replica", None, None, None),
            P("section", "replica", None, None),
        ),
        check_vma=False,
    )
```

```python
import jax
import jax.numpy as jnp
from jax import lax
from jax.experimental import pallas as pl
from jax.experimental.pallas import tpu as pltpu
from jax.sharding import PartitionSpec as P

EPS = 1e-06
BETA = 0.9
MESH = pl.DeviceIdType.MESH
F32, BF16 = jnp.float32, jnp.bfloat16
SECTIONS, REPLICAS, MICRO, ROWS, D, FF, BUCKET = 8, 32, 2, 64, 2048, 768, 128
UNITS = 4
UROWS = MICRO * ROWS // UNITS
PR, PC = UROWS // 2, 128
BR, BC = 32, 128
CHUNK = 256
GROUPS = 4
SPAN = D // GROUPS
BP = (BUCKET // BR) * (FF // BC)


def kernel(inp, cot, gate_h, up_h, down_h, mom_h, routes_v, routes_s, pairing_s,
           act_h, ig_h, buck_h,
           gate, up, down, mom, gx, xd, out, p1, sel, snd, pb, snb, nbuf, rinv_b, g_b, u_b, a_b, b_b, total,
           fresh, partner, bucket, inv_v, inv_s,
           gate_t, up_t, down_t,
           w_sem, m_sem, g_sem, gs_sem, p1_recv, p1_send, p2_recv, p2_send, pb_recv, pb_send, b_recv, snb_send, o_sem, i_sem):
    t = lax.axis_index("section")
    r = lax.axis_index("replica")
    across = lax.rem(t + 4, SECTIONS)
    core, ry, rz = lax.rem(r, 2), r // 8, lax.rem(r, 8) // 2
    group = lax.rem(rz - ry + 4, 4)
    half = lax.rem(ry, 2)
    col = 2 * (2 * group + core) + ry // 2
    fwd_source = lax.rem(t + 4 - core, SECTIONS)
    bwd_source = lax.rem(t + 4 + core, SECTIONS)

    def dev(s, q):
        return {"section": s, "replica": q}

    def wait(ref, sem):
        pltpu.make_async_copy(ref, ref, sem).wait()

    early = t < SECTIONS // 2

    loads = [pltpu.make_async_copy(h, v, w_sem.at[i])
             for i, (h, v) in enumerate(((gate_h.at[0, 0], gate), (up_h.at[0, 0], up), (down_h.at[0, 0], down)))]

    per = SECTIONS * MICRO // UNITS

    def gather(src, goal, sems):
        for m in range(MICRO):
            unit = m * (UNITS // MICRO) + t // per
            place = gx.at[unit, lax.rem(t, per)]

            @pl.when(t == goal)
            def _():
                pltpu.make_async_copy(src.at[0, m], place, g_sem.at[unit]).start()

            @pl.when(t != goal)
            def _():
                pltpu.make_async_remote_copy(
                    src.at[0, m], place, gs_sem.at[sems + m], g_sem.at[unit],
                    device_id=dev(goal, r), device_id_type=MESH).start()

    gather(inp, 0, 0)
    for load in loads:
        load.start()
    gather(cot, SECTIONS - 1, MICRO)
    pltpu.make_async_copy(mom_h.at[0, 0], mom, m_sem).start()

    rv = routes_v[jnp.minimum(fwd_source, SECTIONS - 2)]
    goal_id = lax.broadcasted_iota(jnp.int32, (REPLICAS, REPLICAS), 0)
    from_id = lax.broadcasted_iota(jnp.int32, (REPLICAS, REPLICAS), 1)
    for m in range(MICRO):
        hit = rv[m:m + 1, :] == goal_id
        back = jnp.max(jnp.where(hit, from_id, 0), axis=1, keepdims=True)
        inv_v[m] = jnp.broadcast_to(back, (REPLICAS, 128))
    copy = pltpu.make_async_copy(inv_v, inv_s, i_sem)
    copy.start()
    copy.wait()

    def assemble(m, slot):
        wait(gx.at[m], g_sem.at[m])
        for k in range(per):
            xd[slot, pl.ds(8 * k, 8), :] = gx[m, k]

    def send_chunk(slot, j, step):
        at = across if j % 2 == 0 else lax.rem(t + 4 + step, SECTIONS)
        for k in range(4):
            c, h = 2 * j + k // 2, k % 2
            q = k * 8 + (j // 2 + k) % 4 * 2 + j % 2
            pltpu.make_async_remote_copy(
                out.at[slot, pl.ds(h * PR, PR), pl.ds(c * PC, PC)],
                p1.at[slot, r], p1_send.at[slot], p1_recv.at[slot],
                device_id=dev(at, q), device_id_type=MESH).start()

    def rows_of(m):
        return pl.ds(pl.multiple_of(lax.rem(m, 2) * UROWS, UROWS), UROWS)

    def forward(m):
        @pl.when(t == 0)
        def _():
            assemble(m, m)

        @pl.when(jnp.logical_and(m == 0, early))
        def _():
            loads[0].wait()
            loads[1].wait()

        squares = jnp.zeros((UROWS, 128), F32)
        g = jnp.zeros((UROWS, FF), F32)
        u = jnp.zeros((UROWS, FF), F32)
        for k in range(GROUPS):
            cols = pl.ds(k * SPAN, SPAN)

            @pl.when(t != 0)
            def _():
                wait(xd.at[m, :, cols], p2_recv.at[m, k])

            a = xd[m, :, cols]
            g = g + jnp.dot(a, gate[cols, :], preferred_element_type=F32)
            u = u + jnp.dot(a, up[cols, :], preferred_element_type=F32)
            for c in range(0, SPAN, 128):
                af = a[:, c:c + 128].astype(F32)
                squares = squares + af * af
        rinv = lax.rsqrt(jnp.sum(squares, axis=-1, keepdims=True) * (1.0 / D) + EPS)
        g = g * rinv
        u = u * rinv
        sg = jax.nn.sigmoid(g)
        gs = g * sg
        hidden = (gs * u).astype(BF16)

        @pl.when(jnp.logical_and(m == 0, early))
        def _():
            loads[2].wait()

        for c in range(0, D, CHUNK):
            res = xd[m, :, pl.ds(c, CHUNK)].astype(F32) + jnp.dot(
                hidden, down[:, pl.ds(c, CHUNK)], preferred_element_type=F32)
            out[m, :, pl.ds(c, CHUNK)] = res.astype(BF16)

            @pl.when(t < SECTIONS - 1)
            def _():
                send_chunk(m, c // CHUNK, 1)

        pltpu.make_async_copy(out.at[m], act_h.at[0, 0, m // 2, rows_of(m), :], o_sem).start()
        rinv_b[m] = jnp.broadcast_to(rinv, (UROWS, 128))
        nbuf[m] = (xd[m, :, :BUCKET].astype(F32) * rinv).astype(BF16)
        g_b[m] = g
        u_b[m] = u
        a_b[m] = u * sg * (1.0 + g * (1.0 - sg))
        b_b[m] = gs

    def backward(m):
        slot = UNITS + m

        @pl.when(t == SECTIONS - 1)
        def _():
            assemble(m, slot)

        dh = jnp.zeros((UROWS, FF), F32)
        for k in range(GROUPS):
            cols = pl.ds(k * SPAN, SPAN)

            @pl.when(t != SECTIONS - 1)
            def _():
                wait(xd.at[slot, :, cols], p2_recv.at[slot, k])

            dh = dh + jnp.dot(xd[slot, :, cols], down_t[cols, :], preferred_element_type=F32)
        dg = (dh * a_b[m]).astype(BF16)
        du = (dh * b_b[m]).astype(BF16)
        both = dg.astype(F32) * g_b[m] + du.astype(F32) * u_b[m]
        corr = jnp.sum(both, axis=-1, keepdims=True) * (1.0 / D)
        rinv = rinv_b[m][:, :1]
        for c in range(0, D, CHUNK):
            cols = pl.ds(c, CHUNK)
            dn = jnp.dot(dg, gate_t[:, cols], preferred_element_type=F32) + jnp.dot(
                du, up_t[:, cols], preferred_element_type=F32)
            n = xd[m, :, pl.ds(c, CHUNK)].astype(F32) * rinv
            res = xd[slot, :, pl.ds(c, CHUNK)].astype(F32) + rinv * (dn - n * corr)
            out[slot, :, pl.ds(c, CHUNK)] = res.astype(BF16)

            @pl.when(t > 0)
            def _():
                send_chunk(slot, c // CHUNK, -1)

        pltpu.make_async_copy(out.at[slot], ig_h.at[0, 0, m // 2, rows_of(m), :], o_sem).start()
        part = lax.dot_general(nbuf[m], dg, (((0,), (0,)), ((), ())), preferred_element_type=F32)

        total[...] = total[...] + part

    def relay(slot, goal, index):
        wait(p1.at[slot], p1_recv.at[slot])
        sel[...] = p1[slot]
        place = xd.at[slot, pl.ds(pl.multiple_of(half * PR, PR), PR), pl.ds(pl.multiple_of(col * PC, PC), PC)]

        def body(d, carry):
            snd[slot, d] = sel[index(d)]
            pltpu.make_async_remote_copy(
                snd.at[slot, d], place, p2_send.at[slot], p2_recv.at[slot, group],
                device_id=dev(goal, d), device_id_type=MESH).start()
            return carry

        lax.fori_loop(0, REPLICAS, body, 0, unroll=8)

    def loop(body):
        def step(m, carry):
            body(m)
            return carry

        lax.fori_loop(0, UNITS, step, 0)

    def relay_forward():
        @pl.when(fwd_source < SECTIONS - 1)
        def _():
            loop(lambda m: relay(m, fwd_source + 1, lambda d: inv_s[m // 2, d, 0]))

    def relay_backward():
        @pl.when(bwd_source > 0)
        def _():
            loop(lambda m: relay(UNITS + m, bwd_source - 1, lambda d: routes_s[bwd_source - 1, m // 2, d]))

    def relay_bucket():
        @pl.when(r < BP)
        def _():
            wait(pb, pb_recv)
            brow, bcol = r // (FF // BC), lax.rem(r, FF // BC)
            place = partner.at[pl.ds(pl.multiple_of(brow * BR, BR), BR), pl.ds(pl.multiple_of(bcol * BC, BC), BC)]

            def body(d, carry):
                snb[d] = pb[pairing_s[across, d]]
                pltpu.make_async_remote_copy(
                    snb.at[d], place, snb_send, b_recv,
                    device_id=dev(across, d), device_id_type=MESH).start()
                return carry

            lax.fori_loop(0, REPLICAS, body, 0, unroll=4)

    def transpose():
        def body(i, carry):
            cols = pl.ds(pl.multiple_of(i * CHUNK, CHUNK), CHUNK)
            gate_t[:, cols] = gate[cols, :].T
            up_t[:, cols] = up[cols, :].T
            down_t[cols, :] = down[:, cols].T
            return carry

        lax.fori_loop(0, D // CHUNK, body, 0)

    total[...] = jnp.zeros_like(total)

    @pl.when(jnp.logical_not(early))
    def _():
        relay_forward()
        for load in loads:
            load.wait()
        transpose()

    last = t == SECTIONS - 1

    def step(i, carry):
        ahead = jnp.where(last, lax.rem(i, 2) == 0, i < UNITS)
        m = jnp.where(last, i // 2, lax.rem(i, UNITS))

        @pl.when(jnp.logical_and(i == UNITS, early))
        def _():
            transpose()
            relay_forward()
            relay_backward()
            relay_bucket()

        @pl.when(ahead)
        def _():
            forward(m)

        @pl.when(jnp.logical_not(ahead))
        def _():
            backward(m)

        return carry

    lax.fori_loop(0, 2 * UNITS, step, 0)

    wait(mom, m_sem)
    fresh[...] = (BETA * mom[...] + (1.0 - BETA) * total[...]).astype(BF16)
    for q in range(BP):
        pltpu.make_async_remote_copy(
            fresh.at[pl.ds(q // (FF // BC) * BR, BR), pl.ds(q % (FF // BC) * BC, BC)],
            pb.at[r], pb_send, pb_recv,
            device_id=dev(across, q), device_id_type=MESH).start()

    @pl.when(jnp.logical_not(early))
    def _():
        relay_backward()
        relay_bucket()

    wait(partner, b_recv)
    bucket[...] = 0.5 * (fresh[...].astype(F32) + partner[...].astype(F32))
    pltpu.make_async_copy(bucket, buck_h.at[0, 0], m_sem).start()

    wait(fresh, pb_send)

    @pl.when(r < BP)
    def _():
        wait(snb, snb_send)

    @pl.when(t < SECTIONS - 1)
    def _():
        loop(lambda m: wait(out.at[m], p1_send.at[m]))

    @pl.when(t > 0)
    def _():
        loop(lambda m: wait(out.at[UNITS + m], p1_send.at[UNITS + m]))

    @pl.when(fwd_source < SECTIONS - 1)
    def _():
        loop(lambda m: wait(snd.at[m], p2_send.at[m]))

    @pl.when(bwd_source > 0)
    def _():
        loop(lambda m: wait(snd.at[UNITS + m], p2_send.at[UNITS + m]))

    def sent(src, sems):
        for m in range(MICRO):
            pltpu.make_async_remote_copy(
                src.at[0, m], gx.at[0, 0], gs_sem.at[sems + m], g_sem.at[0],
                device_id=dev(0, r), device_id_type=MESH).wait_send()

    @pl.when(t != 0)
    def _():
        sent(inp, 0)

    @pl.when(t != SECTIONS - 1)
    def _():
        sent(cot, MICRO)

    wait(out, o_sem)
    wait(bucket, m_sem)


def hand_over(*refs):
    came, made, held, sem = refs[:3], refs[3:6], refs[6:9], refs[9]
    into = [pltpu.make_async_copy(came[i], held[i], sem.at[i]) for i in range(3)]
    away = [pltpu.make_async_copy(held[i], made[i], sem.at[3 + i]) for i in range(3)]
    for copy in into:
        copy.start()
    for i in range(3):
        into[i].wait()
        away[i].start()
    for copy in away:
        copy.wait()


def local(inputs, cotangent, gate_weight, up_weight, down_weight, momentum, routes, pairing):
    hbm = pl.BlockSpec(memory_space=pl.ANY)
    smem = pl.BlockSpec(memory_space=pltpu.SMEM)
    vmem = pl.BlockSpec(memory_space=pltpu.VMEM)
    dma = pltpu.SemaphoreType.DMA
    slots = 2 * UNITS
    made = pl.pallas_call(
        kernel,
        out_shape=(
            jax.ShapeDtypeStruct((1, 1, MICRO, ROWS, D), BF16),
            jax.ShapeDtypeStruct((1, 1, MICRO, ROWS, D), BF16),
            jax.ShapeDtypeStruct((1, 1, BUCKET, FF), F32),
        ),
        in_specs=[hbm] * 6 + [vmem, smem, smem],
        out_specs=(hbm, hbm, hbm),
        scratch_shapes=[
            pltpu.VMEM((D, FF), BF16),
            pltpu.VMEM((D, FF), BF16),
            pltpu.VMEM((FF, D), BF16),
            pltpu.VMEM((BUCKET, FF), F32),
            pltpu.VMEM((UNITS, SECTIONS * MICRO // UNITS, ROWS // SECTIONS, D), BF16),
            pltpu.VMEM((slots, UROWS, D), BF16),
            pltpu.VMEM((slots, UROWS, D), BF16),
            pltpu.VMEM((slots, REPLICAS, PR, PC), BF16),
            pltpu.VMEM((REPLICAS, PR, PC), BF16),
            pltpu.VMEM((slots, REPLICAS, PR, PC), BF16),
            pltpu.VMEM((REPLICAS, BR, BC), BF16),
            pltpu.VMEM((REPLICAS, BR, BC), BF16),
            pltpu.VMEM((UNITS, UROWS, BUCKET), BF16),
            pltpu.VMEM((UNITS, UROWS, 128), F32),
            *[pltpu.VMEM((UNITS, UROWS, FF), F32)] * 4,
            pltpu.VMEM((BUCKET, FF), F32),
            pltpu.VMEM((BUCKET, FF), BF16),
            pltpu.VMEM((BUCKET, FF), BF16),
            pltpu.VMEM((BUCKET, FF), F32),
            pltpu.VMEM((MICRO, REPLICAS, 128), jnp.int32),
            pltpu.SMEM((MICRO, REPLICAS, 128), jnp.int32),
            pltpu.VMEM((FF, D), BF16),
            pltpu.VMEM((FF, D), BF16),
            pltpu.VMEM((D, FF), BF16),
            dma((3,)),
            dma,
            dma((UNITS,)),
            dma((2 * MICRO,)),
            dma((slots,)),
            dma((slots,)),
            dma((slots, GROUPS)),
            dma((slots,)),
            *[dma] * 6,
        ],
        compiler_params=pltpu.CompilerParams(has_side_effects=True, vmem_limit_bytes=56 << 20),
    )(inputs, cotangent, gate_weight, up_weight, down_weight, momentum, routes, routes, pairing)
    return pl.pallas_call(
        hand_over,
        out_shape=tuple(jax.ShapeDtypeStruct(a.shape, a.dtype) for a in made),
        in_specs=[hbm] * 3,
        out_specs=(hbm, hbm, hbm),
        scratch_shapes=[*[pltpu.VMEM(a.shape, a.dtype) for a in made], dma((6,))],
    )(*made)


def solution(mesh):
    placed = (
        P("replica", None, "section", None),
        P("replica", None, "section", None),
        P("section", "replica", None, None),
        P("section", "replica", None, None),
        P("section", "replica", None, None),
        P("section", "replica", None, None),
        P(),
        P(),
    )
    return jax.shard_map(
        local,
        mesh=mesh,
        in_specs=placed,
        out_specs=(
            P("section", "replica", None, None, None),
            P("section", "replica", None, None, None),
            P("section", "replica", None, None),
        ),
        check_vma=False,
    )
```

```python
import jax
import jax.numpy as jnp
from jax import lax
from jax.experimental import pallas as pl
from jax.experimental.pallas import tpu as pltpu
from jax.sharding import PartitionSpec as P

EPS = 1e-06
BETA = 0.9
MESH = pl.DeviceIdType.MESH
F32, BF16 = jnp.float32, jnp.bfloat16
SECTIONS, REPLICAS, MICRO, ROWS, D, FF, BUCKET = 8, 32, 2, 64, 2048, 768, 128
UNITS = 4
UROWS = MICRO * ROWS // UNITS
PR, PC = UROWS // 2, 128
BR, BC = 32, 128
CHUNK = 256
GROUPS = 4
SPAN = D // GROUPS
BP = (BUCKET // BR) * (FF // BC)


def kernel(inp, cot, gate_h, up_h, down_h, mom_h, routes_v, routes_s, pairing_s,
           act_h, ig_h, buck_h,
           gate, up, down, mom, gx, xd, out, p1, sel, snd, pb, snb, nbuf, rinv_b, g_b, u_b, a_b, b_b, total,
           fresh, partner, bucket, inv_v, inv_s,
           gate_t, up_t, down_t,
           w_sem, m_sem, g_sem, gs_sem, p1_recv, p1_send, p2_recv, p2_send, pb_recv, pb_send, b_recv, snb_send, o_sem, i_sem):
    t = lax.axis_index("section")
    r = lax.axis_index("replica")
    across = lax.rem(t + 4, SECTIONS)
    core, ry, rz = lax.rem(r, 2), r // 8, lax.rem(r, 8) // 2
    group = lax.rem(rz - ry + 4, 4)
    half = lax.rem(ry, 2)
    col = 2 * (2 * group + core) + ry // 2
    fwd_source = lax.rem(t + 4 - core, SECTIONS)
    bwd_source = lax.rem(t + 4 + core, SECTIONS)

    def dev(s, q):
        return {"section": s, "replica": q}

    def wait(ref, sem):
        pltpu.make_async_copy(ref, ref, sem).wait()

    early = t < SECTIONS // 2

    loads = [pltpu.make_async_copy(h, v, w_sem.at[i])
             for i, (h, v) in enumerate(((gate_h.at[0, 0], gate), (up_h.at[0, 0], up), (down_h.at[0, 0], down)))]

    barrier = pltpu.get_barrier_semaphore()

    def signal(s, q):
        pl.semaphore_signal(barrier, inc=1, device_id=dev(s, q), device_id_type=MESH)

    def greet():
        def body(q, carry):
            for ahead in (3, 4, 5):
                signal(lax.rem(t + ahead, SECTIONS), q)
            return carry

        for end in (0, SECTIONS - 1):
            @pl.when(t != end)
            def _():
                signal(end, r)

            @pl.when(t == end)
            def _():
                for s in range(SECTIONS):
                    if s != end:
                        signal(s, r)

        lax.fori_loop(0, REPLICAS, body, 0, unroll=4)

    per = SECTIONS * MICRO // UNITS

    def gather(src, goal, sems):
        for m in range(MICRO):
            unit = m * (UNITS // MICRO) + t // per
            place = gx.at[unit, lax.rem(t, per)]

            @pl.when(t == goal)
            def _():
                pltpu.make_async_copy(src.at[0, m], place, g_sem.at[unit]).start()

            @pl.when(t != goal)
            def _():
                pltpu.make_async_remote_copy(
                    src.at[0, m], place, gs_sem.at[sems + m], g_sem.at[unit],
                    device_id=dev(goal, r), device_id_type=MESH).start()

    for load in loads:
        load.start()
    pltpu.make_async_copy(mom_h.at[0, 0], mom, m_sem).start()
    greet()
    rv = routes_v[jnp.minimum(fwd_source, SECTIONS - 2)]
    goal_id = lax.broadcasted_iota(jnp.int32, (REPLICAS, REPLICAS), 0)
    from_id = lax.broadcasted_iota(jnp.int32, (REPLICAS, REPLICAS), 1)
    for m in range(MICRO):
        hit = rv[m:m + 1, :] == goal_id
        back = jnp.max(jnp.where(hit, from_id, 0), axis=1, keepdims=True)
        inv_v[m] = jnp.broadcast_to(back, (REPLICAS, 128))
    copy = pltpu.make_async_copy(inv_v, inv_s, i_sem)
    copy.start()
    copy.wait()
    pl.semaphore_wait(barrier, jnp.where(jnp.logical_or(t == 0, t == SECTIONS - 1), 3 * REPLICAS + SECTIONS, 3 * REPLICAS + 2))
    gather(inp, 0, 0)
    gather(cot, SECTIONS - 1, MICRO)


    def assemble(m, slot):
        wait(gx.at[m], g_sem.at[m])
        for k in range(per):
            xd[slot, pl.ds(8 * k, 8), :] = gx[m, k]

    def send_chunk(slot, j, step):
        at = across if j % 2 == 0 else lax.rem(t + 4 + step, SECTIONS)
        for k in range(4):
            c, h = 2 * j + k // 2, k % 2
            q = k * 8 + (j // 2 + k) % 4 * 2 + j % 2
            pltpu.make_async_remote_copy(
                out.at[slot, pl.ds(h * PR, PR), pl.ds(c * PC, PC)],
                p1.at[slot, r], p1_send.at[slot], p1_recv.at[slot],
                device_id=dev(at, q), device_id_type=MESH).start()

    def rows_of(m):
        return pl.ds(pl.multiple_of(lax.rem(m, 2) * UROWS, UROWS), UROWS)

    def forward(m):
        @pl.when(t == 0)
        def _():
            assemble(m, m)

        @pl.when(jnp.logical_and(m == 0, early))
        def _():
            loads[0].wait()
            loads[1].wait()

        squares = jnp.zeros((UROWS, 128), F32)
        g = jnp.zeros((UROWS, FF), F32)
        u = jnp.zeros((UROWS, FF), F32)
        for k in range(GROUPS):
            cols = pl.ds(k * SPAN, SPAN)

            @pl.when(t != 0)
            def _():
                wait(xd.at[m, :, cols], p2_recv.at[m, k])

            a = xd[m, :, cols]
            g = g + jnp.dot(a, gate[cols, :], preferred_element_type=F32)
            u = u + jnp.dot(a, up[cols, :], preferred_element_type=F32)
            for c in range(0, SPAN, 128):
                af = a[:, c:c + 128].astype(F32)
                squares = squares + af * af
        rinv = lax.rsqrt(jnp.sum(squares, axis=-1, keepdims=True) * (1.0 / D) + EPS)
        g = g * rinv
        u = u * rinv
        sg = jax.nn.sigmoid(g)
        gs = g * sg
        hidden = (gs * u).astype(BF16)

        @pl.when(jnp.logical_and(m == 0, early))
        def _():
            loads[2].wait()

        for c in range(0, D, 4 * CHUNK):
            res = xd[m, :, pl.ds(c, 4 * CHUNK)].astype(F32) + jnp.dot(
                hidden, down[:, pl.ds(c, 4 * CHUNK)], preferred_element_type=F32)
            out[m, :, pl.ds(c, 4 * CHUNK)] = res.astype(BF16)

            @pl.when(t < SECTIONS - 1)
            def _():
                for o in range(4):
                    send_chunk(m, c // CHUNK + o, 1)

        pltpu.make_async_copy(out.at[m], act_h.at[0, 0, m // 2, rows_of(m), :], o_sem).start()
        rinv_b[m] = jnp.broadcast_to(rinv, (UROWS, 128))
        nbuf[m] = (xd[m, :, :BUCKET].astype(F32) * rinv).astype(BF16)
        g_b[m] = g
        u_b[m] = u
        a_b[m] = u * sg * (1.0 + g * (1.0 - sg))
        b_b[m] = gs

    def accumulate(m, dg):
        total[...] = total[...] + lax.dot_general(
            nbuf[m], dg, (((0,), (0,)), ((), ())), preferred_element_type=F32)

    def send_bucket():
        wait(mom, m_sem)
        fresh[...] = (BETA * mom[...] + (1.0 - BETA) * total[...]).astype(BF16)
        for q in range(BP):
            pltpu.make_async_remote_copy(
                fresh.at[pl.ds(q // (FF // BC) * BR, BR), pl.ds(q % (FF // BC) * BC, BC)],
                pb.at[r], pb_send, pb_recv,
                device_id=dev(across, q), device_id_type=MESH).start()

    def backward(m):
        slot = UNITS + m

        @pl.when(t == SECTIONS - 1)
        def _():
            assemble(m, slot)

        dh = jnp.zeros((UROWS, FF), F32)
        for k in range(GROUPS):
            cols = pl.ds(k * SPAN, SPAN)

            @pl.when(t != SECTIONS - 1)
            def _():
                wait(xd.at[slot, :, cols], p2_recv.at[slot, k])

            dh = dh + jnp.dot(xd[slot, :, cols], down_t[cols, :], preferred_element_type=F32)
        dg = (dh * a_b[m]).astype(BF16)
        du = (dh * b_b[m]).astype(BF16)

        @pl.when(t == 0)
        def _():
            accumulate(m, dg)

        @pl.when(jnp.logical_and(t == 0, m == UNITS - 1))
        def _():
            send_bucket()

        both = dg.astype(F32) * g_b[m] + du.astype(F32) * u_b[m]
        corr = jnp.sum(both, axis=-1, keepdims=True) * (1.0 / D)
        rinv = rinv_b[m][:, :1]
        for c in range(0, D, 4 * CHUNK):
            cols = pl.ds(c, 4 * CHUNK)
            dn = jnp.dot(dg, gate_t[:, cols], preferred_element_type=F32) + jnp.dot(
                du, up_t[:, cols], preferred_element_type=F32)
            n = xd[m, :, pl.ds(c, 4 * CHUNK)].astype(F32) * rinv
            res = xd[slot, :, pl.ds(c, 4 * CHUNK)].astype(F32) + rinv * (dn - n * corr)
            out[slot, :, pl.ds(c, 4 * CHUNK)] = res.astype(BF16)

            @pl.when(t > 0)
            def _():
                for o in range(4):
                    send_chunk(slot, c // CHUNK + o, -1)

        pltpu.make_async_copy(out.at[slot], ig_h.at[0, 0, m // 2, rows_of(m), :], o_sem).start()

        @pl.when(t != 0)
        def _():
            accumulate(m, dg)

    def relay(slot, goal, index):
        wait(p1.at[slot], p1_recv.at[slot])
        sel[...] = p1[slot]
        place = xd.at[slot, pl.ds(pl.multiple_of(half * PR, PR), PR), pl.ds(pl.multiple_of(col * PC, PC), PC)]

        def body(i, carry):
            d = lax.rem(i + r, REPLICAS)
            snd[slot, d] = sel[index(d)]
            pltpu.make_async_remote_copy(
                snd.at[slot, d], place, p2_send.at[slot], p2_recv.at[slot, group],
                device_id=dev(goal, d), device_id_type=MESH).start()
            return carry

        lax.fori_loop(0, REPLICAS, body, 0, unroll=8)

    def loop(body):
        def step(m, carry):
            body(m)
            return carry

        lax.fori_loop(0, UNITS, step, 0)

    def relay_forward():
        @pl.when(fwd_source < SECTIONS - 1)
        def _():
            loop(lambda m: relay(m, fwd_source + 1, lambda d: inv_s[m // 2, d, 0]))

    def relay_backward():
        @pl.when(bwd_source > 0)
        def _():
            loop(lambda m: relay(UNITS + m, bwd_source - 1, lambda d: routes_s[bwd_source - 1, m // 2, d]))

    def relay_bucket():
        @pl.when(r < BP)
        def _():
            wait(pb, pb_recv)
            brow, bcol = r // (FF // BC), lax.rem(r, FF // BC)
            place = partner.at[pl.ds(pl.multiple_of(brow * BR, BR), BR), pl.ds(pl.multiple_of(bcol * BC, BC), BC)]

            def body(d, carry):
                snb[d] = pb[pairing_s[across, d]]
                pltpu.make_async_remote_copy(
                    snb.at[d], place, snb_send, b_recv,
                    device_id=dev(across, d), device_id_type=MESH).start()
                return carry

            lax.fori_loop(0, REPLICAS, body, 0, unroll=4)

    def transpose():
        def body(i, carry):
            cols = pl.ds(pl.multiple_of(i * CHUNK, CHUNK), CHUNK)
            gate_t[:, cols] = gate[cols, :].T
            up_t[:, cols] = up[cols, :].T
            down_t[cols, :] = down[:, cols].T
            return carry

        lax.fori_loop(0, D // CHUNK, body, 0)

    total[...] = jnp.zeros_like(total)

    @pl.when(jnp.logical_not(early))
    def _():
        relay_forward()
        for load in loads:
            load.wait()
        transpose()

    last = t == SECTIONS - 1

    def step(i, carry):
        ahead = jnp.where(last, lax.rem(i, 2) == 0, i < UNITS)
        m = jnp.where(last, i // 2, lax.rem(i, UNITS))

        @pl.when(jnp.logical_and(i == UNITS, early))
        def _():
            transpose()
            relay_forward()
            relay_backward()
            relay_bucket()

        @pl.when(ahead)
        def _():
            forward(m)

        @pl.when(jnp.logical_not(ahead))
        def _():
            backward(m)

        return carry

    lax.fori_loop(0, 2 * UNITS, step, 0)

    @pl.when(t != 0)
    def _():
        send_bucket()

    @pl.when(jnp.logical_not(early))
    def _():
        relay_backward()
        relay_bucket()

    wait(partner, b_recv)
    bucket[...] = 0.5 * (fresh[...].astype(F32) + partner[...].astype(F32))
    pltpu.make_async_copy(bucket, buck_h.at[0, 0], m_sem).start()

    wait(fresh, pb_send)

    @pl.when(r < BP)
    def _():
        wait(snb, snb_send)

    @pl.when(t < SECTIONS - 1)
    def _():
        loop(lambda m: wait(out.at[m], p1_send.at[m]))

    @pl.when(t > 0)
    def _():
        loop(lambda m: wait(out.at[UNITS + m], p1_send.at[UNITS + m]))

    @pl.when(fwd_source < SECTIONS - 1)
    def _():
        loop(lambda m: wait(snd.at[m], p2_send.at[m]))

    @pl.when(bwd_source > 0)
    def _():
        loop(lambda m: wait(snd.at[UNITS + m], p2_send.at[UNITS + m]))

    def sent(src, sems):
        for m in range(MICRO):
            pltpu.make_async_remote_copy(
                src.at[0, m], gx.at[0, 0], gs_sem.at[sems + m], g_sem.at[0],
                device_id=dev(0, r), device_id_type=MESH).wait_send()

    @pl.when(t != 0)
    def _():
        sent(inp, 0)

    @pl.when(t != SECTIONS - 1)
    def _():
        sent(cot, MICRO)

    wait(out, o_sem)
    wait(bucket, m_sem)


def hand_over(*refs):
    came, made, held, sem = refs[:3], refs[3:6], refs[6:9], refs[9]
    into = [pltpu.make_async_copy(came[i], held[i], sem.at[i]) for i in range(3)]
    away = [pltpu.make_async_copy(held[i], made[i], sem.at[3 + i]) for i in range(3)]
    for copy in into:
        copy.start()
    for i in range(3):
        into[i].wait()
        away[i].start()
    for copy in away:
        copy.wait()


def local(inputs, cotangent, gate_weight, up_weight, down_weight, momentum, routes, pairing):
    hbm = pl.BlockSpec(memory_space=pl.ANY)
    smem = pl.BlockSpec(memory_space=pltpu.SMEM)
    vmem = pl.BlockSpec(memory_space=pltpu.VMEM)
    dma = pltpu.SemaphoreType.DMA
    slots = 2 * UNITS
    made = pl.pallas_call(
        kernel,
        out_shape=(
            jax.ShapeDtypeStruct((1, 1, MICRO, ROWS, D), BF16),
            jax.ShapeDtypeStruct((1, 1, MICRO, ROWS, D), BF16),
            jax.ShapeDtypeStruct((1, 1, BUCKET, FF), F32),
        ),
        in_specs=[hbm] * 6 + [vmem, smem, smem],
        out_specs=(hbm, hbm, hbm),
        scratch_shapes=[
            pltpu.VMEM((D, FF), BF16),
            pltpu.VMEM((D, FF), BF16),
            pltpu.VMEM((FF, D), BF16),
            pltpu.VMEM((BUCKET, FF), F32),
            pltpu.VMEM((UNITS, SECTIONS * MICRO // UNITS, ROWS // SECTIONS, D), BF16),
            pltpu.VMEM((slots, UROWS, D), BF16),
            pltpu.VMEM((slots, UROWS, D), BF16),
            pltpu.VMEM((slots, REPLICAS, PR, PC), BF16),
            pltpu.VMEM((REPLICAS, PR, PC), BF16),
            pltpu.VMEM((slots, REPLICAS, PR, PC), BF16),
            pltpu.VMEM((REPLICAS, BR, BC), BF16),
            pltpu.VMEM((REPLICAS, BR, BC), BF16),
            pltpu.VMEM((UNITS, UROWS, BUCKET), BF16),
            pltpu.VMEM((UNITS, UROWS, 128), F32),
            *[pltpu.VMEM((UNITS, UROWS, FF), F32)] * 4,
            pltpu.VMEM((BUCKET, FF), F32),
            pltpu.VMEM((BUCKET, FF), BF16),
            pltpu.VMEM((BUCKET, FF), BF16),
            pltpu.VMEM((BUCKET, FF), F32),
            pltpu.VMEM((MICRO, REPLICAS, 128), jnp.int32),
            pltpu.SMEM((MICRO, REPLICAS, 128), jnp.int32),
            pltpu.VMEM((FF, D), BF16),
            pltpu.VMEM((FF, D), BF16),
            pltpu.VMEM((D, FF), BF16),
            dma((3,)),
            dma,
            dma((UNITS,)),
            dma((2 * MICRO,)),
            dma((slots,)),
            dma((slots,)),
            dma((slots, GROUPS)),
            dma((slots,)),
            *[dma] * 6,
        ],
        compiler_params=pltpu.CompilerParams(collective_id=0, has_side_effects=True, vmem_limit_bytes=56 << 20),
    )(inputs, cotangent, gate_weight, up_weight, down_weight, momentum, routes, routes, pairing)
    return pl.pallas_call(
        hand_over,
        out_shape=tuple(jax.ShapeDtypeStruct(a.shape, a.dtype) for a in made),
        in_specs=[hbm] * 3,
        out_specs=(hbm, hbm, hbm),
        scratch_shapes=[*[pltpu.VMEM(a.shape, a.dtype) for a in made], dma((6,))],
    )(*made)


def solution(mesh):
    placed = (
        P("replica", None, "section", None),
        P("replica", None, "section", None),
        P("section", "replica", None, None),
        P("section", "replica", None, None),
        P("section", "replica", None, None),
        P("section", "replica", None, None),
        P(),
        P(),
    )
    return jax.shard_map(
        local,
        mesh=mesh,
        in_specs=placed,
        out_specs=(
            P("section", "replica", None, None, None),
            P("section", "replica", None, None, None),
            P("section", "replica", None, None),
        ),
        check_vma=False,
    )
```

```python
import jax
import jax.numpy as jnp
from jax import lax
from jax.experimental import pallas as pl
from jax.experimental.pallas import tpu as pltpu
from jax.sharding import PartitionSpec as P

EPS = 1e-06
BETA = 0.9
MESH = pl.DeviceIdType.MESH
F32, BF16 = jnp.float32, jnp.bfloat16
SECTIONS, REPLICAS, MICRO, ROWS, D, FF, BUCKET = 8, 32, 2, 64, 2048, 768, 128
UNITS = 4
UROWS = MICRO * ROWS // UNITS
PR, PC = UROWS // 2, 128
BR, BC = 32, 128
CHUNK = 256
GROUPS = 4
SPAN = D // GROUPS
BP = (BUCKET // BR) * (FF // BC)


def kernel(inp, cot, gate_h, up_h, down_h, mom_h, routes_v, routes_s, pairing_s,
           act_h, ig_h, buck_h,
           gate, up, down, mom, gx, xd, out, p1, sel, snd, pb, snb, nbuf, rinv_b, g_b, u_b, a_b, b_b, total,
           fresh, partner, bucket, inv_v, inv_s,
           gate_t, up_t, down_t,
           w_sem, m_sem, g_sem, gs_sem, p1_recv, p1_send, p2_recv, p2_send, pb_recv, pb_send, b_recv, snb_send, o_sem, i_sem):
    t = lax.axis_index("section")
    r = lax.axis_index("replica")
    across = lax.rem(t + 4, SECTIONS)
    core, ry, rz = lax.rem(r, 2), r // 8, lax.rem(r, 8) // 2
    group = lax.rem(rz - ry + 4, 4)
    half = lax.rem(ry, 2)
    col = 2 * (2 * group + core) + ry // 2
    fwd_source = lax.rem(t + 4 - core, SECTIONS)
    bwd_source = lax.rem(t + 4 + core, SECTIONS)

    def dev(s, q):
        return {"section": s, "replica": q}

    def wait(ref, sem):
        pltpu.make_async_copy(ref, ref, sem).wait()

    early = t < SECTIONS // 2

    loads = [pltpu.make_async_copy(h, v, w_sem.at[i])
             for i, (h, v) in enumerate(((gate_h.at[0, 0], gate), (up_h.at[0, 0], up), (down_h.at[0, 0], down)))]

    barrier = pltpu.get_barrier_semaphore()

    def signal(s, q):
        pl.semaphore_signal(barrier, inc=1, device_id=dev(s, q), device_id_type=MESH)

    def greet():
        def body(q, carry):
            for ahead in (3, 4, 5):
                signal(lax.rem(t + ahead, SECTIONS), q)
            return carry

        for end in (0, SECTIONS - 1):
            @pl.when(t != end)
            def _():
                signal(end, r)

            @pl.when(t == end)
            def _():
                for s in range(SECTIONS):
                    if s != end:
                        signal(s, r)

        lax.fori_loop(0, REPLICAS, body, 0, unroll=4)

    per = SECTIONS * MICRO // UNITS

    def gather(src, goal, sems):
        for m in range(MICRO):
            unit = m * (UNITS // MICRO) + t // per
            place = gx.at[unit, lax.rem(t, per)]

            @pl.when(t == goal)
            def _():
                pltpu.make_async_copy(src.at[0, m], place, g_sem.at[unit]).start()

            @pl.when(t != goal)
            def _():
                pltpu.make_async_remote_copy(
                    src.at[0, m], place, gs_sem.at[sems + m], g_sem.at[unit],
                    device_id=dev(goal, r), device_id_type=MESH).start()

    for load in loads:
        load.start()
    pltpu.make_async_copy(mom_h.at[0, 0], mom, m_sem).start()
    greet()
    rv = routes_v[jnp.minimum(fwd_source, SECTIONS - 2)]
    goal_id = lax.broadcasted_iota(jnp.int32, (REPLICAS, REPLICAS), 0)
    from_id = lax.broadcasted_iota(jnp.int32, (REPLICAS, REPLICAS), 1)
    for m in range(MICRO):
        hit = rv[m:m + 1, :] == goal_id
        back = jnp.max(jnp.where(hit, from_id, 0), axis=1, keepdims=True)
        inv_v[m] = jnp.broadcast_to(back, (REPLICAS, 128))
    copy = pltpu.make_async_copy(inv_v, inv_s, i_sem)
    copy.start()
    copy.wait()
    pl.semaphore_wait(barrier, jnp.where(jnp.logical_or(t == 0, t == SECTIONS - 1), 3 * REPLICAS + SECTIONS, 3 * REPLICAS + 2))
    gather(inp, 0, 0)
    gather(cot, SECTIONS - 1, MICRO)


    def assemble(m, slot):
        wait(gx.at[m], g_sem.at[m])
        for k in range(per):
            xd[slot, pl.ds(8 * k, 8), :] = gx[m, k]

    def send_chunk(slot, j, step):
        at = across if j % 2 == 0 else lax.rem(t + 4 + step, SECTIONS)
        for k in range(4):
            c, h = 2 * j + k // 2, k % 2
            q = k * 8 + (j // 2 + k) % 4 * 2 + j % 2
            pltpu.make_async_remote_copy(
                out.at[slot, pl.ds(h * PR, PR), pl.ds(c * PC, PC)],
                p1.at[slot, r], p1_send.at[slot], p1_recv.at[slot],
                device_id=dev(at, q), device_id_type=MESH).start()

    def rows_of(m):
        return pl.ds(pl.multiple_of(lax.rem(m, 2) * UROWS, UROWS), UROWS)

    def forward(m):
        @pl.when(t == 0)
        def _():
            assemble(m, m)

        @pl.when(jnp.logical_and(m == 0, early))
        def _():
            loads[0].wait()
            loads[1].wait()

        squares = jnp.zeros((UROWS, 128), F32)
        g = jnp.zeros((UROWS, FF), F32)
        u = jnp.zeros((UROWS, FF), F32)
        for k in range(GROUPS):
            cols = pl.ds(k * SPAN, SPAN)

            @pl.when(t != 0)
            def _():
                wait(xd.at[m, :, cols], p2_recv.at[m, k])

            a = xd[m, :, cols]
            g = g + jnp.dot(a, gate[cols, :], preferred_element_type=F32)
            u = u + jnp.dot(a, up[cols, :], preferred_element_type=F32)
            for c in range(0, SPAN, 128):
                af = a[:, c:c + 128].astype(F32)
                squares = squares + af * af
        rinv = lax.rsqrt(jnp.sum(squares, axis=-1, keepdims=True) * (1.0 / D) + EPS)
        g = g * rinv
        u = u * rinv
        sg = jax.nn.sigmoid(g)
        gs = g * sg
        hidden = (gs * u).astype(BF16)

        @pl.when(jnp.logical_and(m == 0, early))
        def _():
            loads[2].wait()

        for c in range(0, D, 4 * CHUNK):
            res = xd[m, :, pl.ds(c, 4 * CHUNK)].astype(F32) + jnp.dot(
                hidden, down[:, pl.ds(c, 4 * CHUNK)], preferred_element_type=F32)
            out[m, :, pl.ds(c, 4 * CHUNK)] = res.astype(BF16)

            @pl.when(t < SECTIONS - 1)
            def _():
                for o in (0, 2, 1, 3):
                    send_chunk(m, c // CHUNK + o, 1)

        pltpu.make_async_copy(out.at[m], act_h.at[0, 0, m // 2, rows_of(m), :], o_sem).start()
        rinv_b[m] = jnp.broadcast_to(rinv, (UROWS, 128))
        nbuf[m] = (xd[m, :, :BUCKET].astype(F32) * rinv).astype(BF16)
        g_b[m] = g
        u_b[m] = u
        a_b[m] = u * sg * (1.0 + g * (1.0 - sg))
        b_b[m] = gs

    def accumulate(m, dg):
        total[...] = total[...] + lax.dot_general(
            nbuf[m], dg, (((0,), (0,)), ((), ())), preferred_element_type=F32)

    def send_bucket():
        wait(mom, m_sem)
        fresh[...] = (BETA * mom[...] + (1.0 - BETA) * total[...]).astype(BF16)
        for q in range(BP):
            pltpu.make_async_remote_copy(
                fresh.at[pl.ds(q // (FF // BC) * BR, BR), pl.ds(q % (FF // BC) * BC, BC)],
                pb.at[r], pb_send, pb_recv,
                device_id=dev(across, q), device_id_type=MESH).start()

    def backward(m):
        slot = UNITS + m

        @pl.when(t == SECTIONS - 1)
        def _():
            assemble(m, slot)

        dh = jnp.zeros((UROWS, FF), F32)
        for k in range(GROUPS):
            cols = pl.ds(k * SPAN, SPAN)

            @pl.when(t != SECTIONS - 1)
            def _():
                wait(xd.at[slot, :, cols], p2_recv.at[slot, k])

            dh = dh + jnp.dot(xd[slot, :, cols], down_t[cols, :], preferred_element_type=F32)
        dg = (dh * a_b[m]).astype(BF16)
        du = (dh * b_b[m]).astype(BF16)

        @pl.when(t == 0)
        def _():
            accumulate(m, dg)

        @pl.when(jnp.logical_and(t == 0, m == UNITS - 1))
        def _():
            send_bucket()

        both = dg.astype(F32) * g_b[m] + du.astype(F32) * u_b[m]
        corr = jnp.sum(both, axis=-1, keepdims=True) * (1.0 / D)
        rinv = rinv_b[m][:, :1]
        for c in range(0, D, 4 * CHUNK):
            cols = pl.ds(c, 4 * CHUNK)
            dn = jnp.dot(dg, gate_t[:, cols], preferred_element_type=F32) + jnp.dot(
                du, up_t[:, cols], preferred_element_type=F32)
            n = xd[m, :, pl.ds(c, 4 * CHUNK)].astype(F32) * rinv
            res = xd[slot, :, pl.ds(c, 4 * CHUNK)].astype(F32) + rinv * (dn - n * corr)
            out[slot, :, pl.ds(c, 4 * CHUNK)] = res.astype(BF16)

            @pl.when(t > 0)
            def _():
                for o in (0, 2, 1, 3):
                    send_chunk(slot, c // CHUNK + o, -1)

        pltpu.make_async_copy(out.at[slot], ig_h.at[0, 0, m // 2, rows_of(m), :], o_sem).start()

        @pl.when(t != 0)
        def _():
            accumulate(m, dg)

    def relay(slot, goal, index):
        wait(p1.at[slot], p1_recv.at[slot])
        sel[...] = p1[slot]
        place = xd.at[slot, pl.ds(pl.multiple_of(half * PR, PR), PR), pl.ds(pl.multiple_of(col * PC, PC), PC)]

        def body(i, carry):
            d = lax.rem(i + r, REPLICAS)
            snd[slot, d] = sel[index(d)]
            pltpu.make_async_remote_copy(
                snd.at[slot, d], place, p2_send.at[slot], p2_recv.at[slot, group],
                device_id=dev(goal, d), device_id_type=MESH).start()
            return carry

        lax.fori_loop(0, REPLICAS, body, 0, unroll=8)

    def loop(body):
        def step(m, carry):
            body(m)
            return carry

        lax.fori_loop(0, UNITS, step, 0)

    def relay_forward():
        @pl.when(fwd_source < SECTIONS - 1)
        def _():
            loop(lambda m: relay(m, fwd_source + 1, lambda d: inv_s[m // 2, d, 0]))

    def relay_backward():
        @pl.when(bwd_source > 0)
        def _():
            loop(lambda m: relay(UNITS + m, bwd_source - 1, lambda d: routes_s[bwd_source - 1, m // 2, d]))

    def relay_bucket():
        @pl.when(r < BP)
        def _():
            wait(pb, pb_recv)
            brow, bcol = r // (FF // BC), lax.rem(r, FF // BC)
            place = partner.at[pl.ds(pl.multiple_of(brow * BR, BR), BR), pl.ds(pl.multiple_of(bcol * BC, BC), BC)]

            def body(d, carry):
                snb[d] = pb[pairing_s[across, d]]
                pltpu.make_async_remote_copy(
                    snb.at[d], place, snb_send, b_recv,
                    device_id=dev(across, d), device_id_type=MESH).start()
                return carry

            lax.fori_loop(0, REPLICAS, body, 0, unroll=4)

    def transpose():
        def body(i, carry):
            cols = pl.ds(pl.multiple_of(i * CHUNK, CHUNK), CHUNK)
            gate_t[:, cols] = gate[cols, :].T
            up_t[:, cols] = up[cols, :].T
            down_t[cols, :] = down[:, cols].T
            return carry

        lax.fori_loop(0, D // CHUNK, body, 0)

    total[...] = jnp.zeros_like(total)

    @pl.when(jnp.logical_not(early))
    def _():
        relay_forward()
        for load in loads:
            load.wait()
        transpose()

    last = t == SECTIONS - 1

    def step(i, carry):
        ahead = jnp.where(last, lax.rem(i, 2) == 0, i < UNITS)
        m = jnp.where(last, i // 2, lax.rem(i, UNITS))

        @pl.when(jnp.logical_and(i == UNITS, early))
        def _():
            transpose()
            relay_forward()
            relay_backward()
            relay_bucket()

        @pl.when(ahead)
        def _():
            forward(m)

        @pl.when(jnp.logical_not(ahead))
        def _():
            backward(m)

        return carry

    lax.fori_loop(0, 2 * UNITS, step, 0)

    @pl.when(t != 0)
    def _():
        send_bucket()

    @pl.when(jnp.logical_not(early))
    def _():
        relay_backward()
        relay_bucket()

    wait(partner, b_recv)
    bucket[...] = 0.5 * (fresh[...].astype(F32) + partner[...].astype(F32))
    pltpu.make_async_copy(bucket, buck_h.at[0, 0], m_sem).start()

    wait(fresh, pb_send)

    @pl.when(r < BP)
    def _():
        wait(snb, snb_send)

    @pl.when(t < SECTIONS - 1)
    def _():
        loop(lambda m: wait(out.at[m], p1_send.at[m]))

    @pl.when(t > 0)
    def _():
        loop(lambda m: wait(out.at[UNITS + m], p1_send.at[UNITS + m]))

    @pl.when(fwd_source < SECTIONS - 1)
    def _():
        loop(lambda m: wait(snd.at[m], p2_send.at[m]))

    @pl.when(bwd_source > 0)
    def _():
        loop(lambda m: wait(snd.at[UNITS + m], p2_send.at[UNITS + m]))

    def sent(src, sems):
        for m in range(MICRO):
            pltpu.make_async_remote_copy(
                src.at[0, m], gx.at[0, 0], gs_sem.at[sems + m], g_sem.at[0],
                device_id=dev(0, r), device_id_type=MESH).wait_send()

    @pl.when(t != 0)
    def _():
        sent(inp, 0)

    @pl.when(t != SECTIONS - 1)
    def _():
        sent(cot, MICRO)

    wait(out, o_sem)
    wait(bucket, m_sem)


def hand_over(*refs):
    came, made, held, sem = refs[:3], refs[3:6], refs[6:9], refs[9]
    into = [pltpu.make_async_copy(came[i], held[i], sem.at[i]) for i in range(3)]
    away = [pltpu.make_async_copy(held[i], made[i], sem.at[3 + i]) for i in range(3)]
    for copy in into:
        copy.start()
    for i in range(3):
        into[i].wait()
        away[i].start()
    for copy in away:
        copy.wait()


def local(inputs, cotangent, gate_weight, up_weight, down_weight, momentum, routes, pairing):
    hbm = pl.BlockSpec(memory_space=pl.ANY)
    smem = pl.BlockSpec(memory_space=pltpu.SMEM)
    vmem = pl.BlockSpec(memory_space=pltpu.VMEM)
    dma = pltpu.SemaphoreType.DMA
    slots = 2 * UNITS
    made = pl.pallas_call(
        kernel,
        out_shape=(
            jax.ShapeDtypeStruct((1, 1, MICRO, ROWS, D), BF16),
            jax.ShapeDtypeStruct((1, 1, MICRO, ROWS, D), BF16),
            jax.ShapeDtypeStruct((1, 1, BUCKET, FF), F32),
        ),
        in_specs=[hbm] * 6 + [vmem, smem, smem],
        out_specs=(hbm, hbm, hbm),
        scratch_shapes=[
            pltpu.VMEM((D, FF), BF16),
            pltpu.VMEM((D, FF), BF16),
            pltpu.VMEM((FF, D), BF16),
            pltpu.VMEM((BUCKET, FF), F32),
            pltpu.VMEM((UNITS, SECTIONS * MICRO // UNITS, ROWS // SECTIONS, D), BF16),
            pltpu.VMEM((slots, UROWS, D), BF16),
            pltpu.VMEM((slots, UROWS, D), BF16),
            pltpu.VMEM((slots, REPLICAS, PR, PC), BF16),
            pltpu.VMEM((REPLICAS, PR, PC), BF16),
            pltpu.VMEM((slots, REPLICAS, PR, PC), BF16),
            pltpu.VMEM((REPLICAS, BR, BC), BF16),
            pltpu.VMEM((REPLICAS, BR, BC), BF16),
            pltpu.VMEM((UNITS, UROWS, BUCKET), BF16),
            pltpu.VMEM((UNITS, UROWS, 128), F32),
            *[pltpu.VMEM((UNITS, UROWS, FF), F32)] * 4,
            pltpu.VMEM((BUCKET, FF), F32),
            pltpu.VMEM((BUCKET, FF), BF16),
            pltpu.VMEM((BUCKET, FF), BF16),
            pltpu.VMEM((BUCKET, FF), F32),
            pltpu.VMEM((MICRO, REPLICAS, 128), jnp.int32),
            pltpu.SMEM((MICRO, REPLICAS, 128), jnp.int32),
            pltpu.VMEM((FF, D), BF16),
            pltpu.VMEM((FF, D), BF16),
            pltpu.VMEM((D, FF), BF16),
            dma((3,)),
            dma,
            dma((UNITS,)),
            dma((2 * MICRO,)),
            dma((slots,)),
            dma((slots,)),
            dma((slots, GROUPS)),
            dma((slots,)),
            *[dma] * 6,
        ],
        compiler_params=pltpu.CompilerParams(collective_id=0, has_side_effects=True, vmem_limit_bytes=56 << 20),
    )(inputs, cotangent, gate_weight, up_weight, down_weight, momentum, routes, routes, pairing)
    return pl.pallas_call(
        hand_over,
        out_shape=tuple(jax.ShapeDtypeStruct(a.shape, a.dtype) for a in made),
        in_specs=[hbm] * 3,
        out_specs=(hbm, hbm, hbm),
        scratch_shapes=[*[pltpu.VMEM(a.shape, a.dtype) for a in made], dma((6,))],
    )(*made)


def solution(mesh):
    placed = (
        P("replica", None, "section", None),
        P("replica", None, "section", None),
        P("section", "replica", None, None),
        P("section", "replica", None, None),
        P("section", "replica", None, None),
        P("section", "replica", None, None),
        P(),
        P(),
    )
    return jax.shard_map(
        local,
        mesh=mesh,
        in_specs=placed,
        out_specs=(
            P("section", "replica", None, None, None),
            P("section", "replica", None, None, None),
            P("section", "replica", None, None),
        ),
        check_vma=False,
    )
```
